256 devices in a mesh: tm: 8 (over x, y_hi), rows: 32 (over y_lo, z, core).
Axes of the slice: x: 4, y: 4 (y_hi: 2, y_lo: 2; y = y_hi * 2 + y_lo), z: 8, core: 2. Of those that a mesh axis runs over, the one named last changes fastest.
Arguments:
- frames_in: bfloat16 [32, 512, 64, 128], P('tm', 'rows'), may hold values from -6 to 6
- conv_one: bfloat16 [64, 3, 3, 64], replicated, may hold values from -0.375 to 0.375
- conv_two: bfloat16 [64, 3, 3, 64], replicated, may hold values from -0.375 to 0.375
- temporal: bfloat16 [3, 64, 64], replicated, may hold values from -0.625 to 0.625
- conv_three: bfloat16 [64, 3, 3, 64], replicated, may hold values from -0.375 to 0.375
- conv_four: bfloat16 [64, 3, 3, 64], replicated, may hold values from -0.375 to 0.375
- cotangent: bfloat16 [32, 512, 64, 128], P('tm', 'rows'), may hold values from -6 to 6
Outputs:
- decoded: bfloat16 [32, 512, 64, 128], P('tm', 'rows')
- grad_in: float32 [32, 512, 64, 128], P('tm', 'rows')
The draws below stay inside these ranges and needn't reach their ends.
All inputs are finite; a program needn't handle non-finite values.
Results may differ from the reference program's by a relative error of at most 0.013.
Values may be sent and summed in bfloat16 or wider, within the bound.
A program may use at most 64 MiB of HBM per device.

```python
import jax
import jax.numpy as jnp
from jax import lax

C = 64
W = 128
FRAMES = 32
NROWS = 512


def level_of(stream_key, shape, shards, smallest, top_value):
    gain, own = 1.0, jax.random.fold_in(stream_key, 6)
    for axis_at, blocks in shards:
        heights = jnp.exp(jax.random.uniform(jax.random.fold_in(own, axis_at), (blocks,), jnp.float32, smallest / len(shards), top_value / len(shards)))
        gain = gain * jnp.repeat(heights, shape[axis_at] // blocks).reshape([-1 if axis == axis_at else 1 for axis in range(len(shape))])
    return gain


def gaussian(own_key, extent, deviation, reach, shards=(), held_as=jnp.bfloat16):
    drawn = deviation * jax.random.normal(own_key, extent, jnp.float32)
    if shards:
        drawn = drawn * level_of(own_key, extent, shards, -0.22, 0.18)
    return jnp.clip(drawn, -reach, reach).astype(held_as)


def setup_inputs(seed: int = 0) -> dict:
    key_list = jax.random.split(jax.random.key(seed), 8)
    return {
        "frames_in": gaussian(key_list[0], (FRAMES, NROWS, C, W), 1.0, 6.0, ((0, 8), (1, 32))),
        "conv_one": gaussian(key_list[1], (C, 3, 3, C), (9 * C // 2) ** -0.5, 0.375),
        "conv_two": gaussian(key_list[2], (C, 3, 3, C), (9 * C // 2) ** -0.5, 0.375),
        "temporal": gaussian(key_list[3], (3, C, C), (3 * C // 2) ** -0.5, 0.625),
        "conv_three": gaussian(key_list[4], (C, 3, 3, C), (9 * C // 2) ** -0.5, 0.375),
        "conv_four": gaussian(key_list[5], (C, 3, 3, C), (9 * C // 2) ** -0.5, 0.375),
        "cotangent": gaussian(key_list[6], (FRAMES, NROWS, C, W), 1.0, 6.0, ((0, 8), (1, 32))),
    }


SQRT_HALF = 0.7071067811865476
INV_ROOT_TAU = 0.3989422804014327


def gelu_value(v):
    return 0.5 * v * (1.0 + jax.scipy.special.erf(v * SQRT_HALF))


def gelu_slope(v):
    return 0.5 * (1.0 + jax.scipy.special.erf(v * SQRT_HALF)) + v * jnp.exp(-0.5 * v * v) * INV_ROOT_TAU


def flipped(kernel):
    return jnp.transpose(kernel[:, ::-1, ::-1, :], (3, 1, 2, 0))


def spatial(source, kernel):
    weights = kernel.reshape(kernel.shape[0], -1).astype(jnp.float32)
    padded = jnp.pad(source, ((0, 0), (1, 1), (0, 0), (1, 1)))
    row_count = source.shape[1]
    span_width = source.shape[3]

    def single(plane):
        columns = jnp.concatenate([plane[tap_row:tap_row + row_count, :, tap_col:tap_col + span_width]
                                   for tap_row in range(3) for tap_col in range(3)], axis=1).astype(jnp.float32)
        return jnp.einsum('ok,rkw->row', weights, columns, precision=lax.Precision.HIGHEST)

    return lax.map(single, padded)


def causal_mix(source, temporal):
    count = source.shape[0]
    padded = jnp.concatenate([jnp.zeros((2,) + source.shape[1:], source.dtype), source], axis=0).astype(jnp.float32)
    weights = temporal.astype(jnp.float32)
    total = jnp.zeros(source.shape, jnp.float32)
    for lag in range(3):
        total = total + jnp.einsum('oc,frcw->frow', weights[lag], padded[lag:lag + count], precision=lax.Precision.HIGHEST)
    return total


def causal_back(source, temporal):
    count = source.shape[0]
    padded = jnp.concatenate([source, jnp.zeros((2,) + source.shape[1:], source.dtype)], axis=0).astype(jnp.float32)
    weights = temporal.astype(jnp.float32)
    total = jnp.zeros(source.shape, jnp.float32)
    for lag in range(3):
        total = total + jnp.einsum('oc,frow->frcw', weights[lag], padded[2 - lag:2 - lag + count], precision=lax.Precision.HIGHEST)
    return total


def reference(frames_in, conv_one, conv_two, temporal, conv_three, conv_four, cotangent):
    pre_one = spatial(frames_in, conv_one)
    act_one = gelu_value(pre_one).astype(jnp.bfloat16)
    pre_two = spatial(act_one, conv_two)
    act_two = gelu_value(pre_two).astype(jnp.bfloat16)
    pre_three = causal_mix(act_two, temporal)
    act_three = gelu_value(pre_three).astype(jnp.bfloat16)
    pre_four = spatial(act_three, conv_three)
    act_four = gelu_value(pre_four).astype(jnp.bfloat16)
    decoded = spatial(act_four, conv_four).astype(jnp.bfloat16)
    back_four = (spatial(cotangent, flipped(conv_four)) * gelu_slope(pre_four)).astype(jnp.bfloat16)
    back_three = (spatial(back_four, flipped(conv_three)) * gelu_slope(pre_three)).astype(jnp.bfloat16)
    back_two = (causal_back(back_three, temporal) * gelu_slope(pre_two)).astype(jnp.bfloat16)
    back_one = (spatial(back_two, flipped(conv_two)) * gelu_slope(pre_one)).astype(jnp.bfloat16)
    grad_in = spatial(back_one, flipped(conv_one))
    return decoded, grad_in
```

```python
import functools

import jax
import jax.numpy as jnp
from jax import lax
from jax.experimental import pallas as pl
from jax.experimental.pallas import tpu as pltpu
from jax.sharding import PartitionSpec as P

SQRT_HALF = 0.7071067811865476
INV_ROOT_TAU = 0.3989422804014327
MESH = pl.DeviceIdType.MESH
C = 64
W = 128
PIECES = ((0, 2), (14, 16), (2, 8), (8, 14))


def gelu_both(v):
    phi = 0.5 + 0.5 * lax.erf(v * SQRT_HALF)
    bump = jnp.exp(v * v * -0.5) * INV_ROOT_TAU
    return v * phi, phi + v * bump


def kernel(sizes, x_hbm, k1, k2, t_hbm, k3, k4, cot_hbm, dec_hbm, grad_hbm,
           x1, xc, x3, x5, act1, sl1, act2, sl2, sl3, act4, bk4, b3, bk1, dec, grad, fw, bw, tf, tb, kraw, traw,
           w_sem, in_sem, out_sem, hs, hr, x3s, x3r, x5s, x5r, a_s, a_r, b_s, b_r):
    n_tm, n_rows, rows = sizes
    tm = lax.axis_index("tm")
    band = lax.axis_index("rows")
    has_up, has_down = band > 0, band < n_rows - 1
    has_prev, has_next = tm > 0, tm < n_tm - 1
    bf16, f32 = jnp.bfloat16, jnp.float32

    w_copies = [pltpu.make_async_copy(k, kraw.at[i], w_sem.at[i]) for i, k in enumerate((k1, k2, k3, k4))]
    w_copies.append(pltpu.make_async_copy(t_hbm, traw, w_sem.at[4]))
    for c in w_copies:
        c.start()

    def load(which, f):
        src, dst = ((x_hbm, x1), (cot_hbm, xc))[which]
        return pltpu.make_async_copy(
            src.at[f], dst.at[f // 2, 2:rows + 2, :, (f % 2) * W:(f % 2 + 1) * W], in_sem.at[which, f])

    for which, f in ((0, 2), (0, 3), (0, 0), (0, 1), (1, 2), (1, 3), (1, 0), (1, 1)):
        load(which, f).start()

    barrier = pltpu.get_barrier_semaphore()
    count = jnp.int32(0)
    for ok, peer in ((has_up, {"rows": band - 1}), (has_down, {"rows": band + 1}),
                     (has_prev, {"tm": tm - 1}), (has_next, {"tm": tm + 1})):
        @pl.when(ok)
        def _():
            pl.semaphore_signal(barrier, inc=1, device_id=peer, device_id_type=MESH)
        count = count + ok.astype(jnp.int32)
    pl.semaphore_wait(barrier, count)

    def border(src_of, dst_of, send, recv, at):
        down = pltpu.make_async_remote_copy(
            src_of(rows - 2), dst_of(0), send.at[*at, 0], recv.at[*at, 0],
            device_id={"rows": band + 1}, device_id_type=MESH)
        up = pltpu.make_async_remote_copy(
            src_of(0), dst_of(rows + 2), send.at[*at, 1], recv.at[*at, 1],
            device_id={"rows": band - 1}, device_id_type=MESH)
        return down, up

    def border_start(copies):
        down, up = copies

        @pl.when(has_down)
        def _():
            down.start()

        @pl.when(has_up)
        def _():
            up.start()

    def border_arrived(copies):
        down, up = copies

        @pl.when(has_up)
        def _():
            down.wait_recv()

        @pl.when(has_down)
        def _():
            up.wait_recv()

    def border_sent(copies):
        down, up = copies

        @pl.when(has_down)
        def _():
            down.wait_send()

        @pl.when(has_up)
        def _():
            up.wait_send()

    def input_border(which, f):
        src, dst = ((x_hbm, x1), (cot_hbm, xc))[which]
        half = slice((f % 2) * W, (f % 2 + 1) * W)
        return border(lambda r: src.at[f, r:r + 2], lambda r: dst.at[f // 2, r:r + 2, :, half], hs, hr, (which, f))

    def pair_border(buf, send, recv, p):
        return border(lambda r: buf.at[p, r + 2:r + 4], lambda r: buf.at[p, r:r + 2], send, recv, (p,))

    for which, f in ((0, 2), (0, 3), (0, 0), (0, 1), (1, 2), (1, 3), (1, 0), (1, 1)):
        border_start(input_border(which, f))

    def a_piece(i):
        lo, hi = PIECES[i]
        return pltpu.make_async_remote_copy(
            act2.at[2, lo:hi], act2.at[0, lo:hi], a_s.at[i], a_r.at[i], device_id={"tm": tm + 1}, device_id_type=MESH)

    def b_piece(i):
        lo, hi = PIECES[i]
        return pltpu.make_async_remote_copy(
            b3.at[0, lo:hi], b3.at[2, lo:hi], b_s.at[i], b_r.at[i], device_id={"tm": tm - 1}, device_id_type=MESH)

    def when_start(ok, copy):
        @pl.when(ok)
        def _():
            copy.start()

    def when_recv(ok, copy):
        @pl.when(ok)
        def _():
            copy.wait_recv()

    def when_sent(ok, copy):
        @pl.when(ok)
        def _():
            copy.wait_send()

    edge = jnp.zeros((2, C, 2 * W), bf16)

    @pl.when(jnp.logical_not(has_up))
    def _():
        for buf in (x1, xc, x3, x5):
            for p in range(2):
                buf[p, 0:2] = edge

    @pl.when(jnp.logical_not(has_down))
    def _():
        for buf in (x1, xc, x3, x5):
            for p in range(2):
                buf[p, rows + 2:rows + 4] = edge

    def clear(ref, at):
        def one(r, _):
            ref[at, r] = edge[0]
            return 0
        lax.fori_loop(0, rows, one, 0)

    @pl.when(jnp.logical_not(has_prev))
    def _():
        clear(act2, 0)

    @pl.when(jnp.logical_not(has_next))
    def _():
        clear(b3, 2)

    def arrange(n):
        w_copies[n].wait()
        for b in range(3):
            blocks = [kraw[n, a, b].astype(f32) for a in range(3)]
            fw[n, b * C:(b + 1) * C, :] = jnp.concatenate(blocks, axis=1).astype(bf16)
            bw[n, (2 - b) * C:(3 - b) * C, :] = jnp.concatenate([k.T for k in blocks[::-1]], axis=1).astype(bf16)

    for n in range(4):
        arrange(n)
    w_copies[4].wait()
    lags = [traw[j].astype(f32) for j in range(3)]
    tf[...] = jnp.concatenate(lags, axis=1).astype(bf16)
    tb[...] = jnp.concatenate([k.T for k in lags[::-1]], axis=1).astype(bf16)

    lane = lax.broadcasted_iota(jnp.int32, (C, W), 1)
    first_lane, last_lane = lane == 0, lane == W - 1

    def conv_row(src, p, weights, r):
        y = jnp.dot(weights, src[p, pl.ds(r, 3)].reshape(3 * C, 2 * W), preferred_element_type=f32)
        out = []
        for q in range(2):
            part = y[:, q * W:(q + 1) * W]
            left = jnp.where(first_lane, 0.0, pltpu.roll(part[0:C], 1, 1))
            right = jnp.where(last_lane, 0.0, pltpu.roll(part[2 * C:], W - 1, 1))
            out.append(left + part[C:2 * C] + right)
        return out

    halves = tuple(enumerate((slice(0, W), slice(W, 2 * W))))

    def loop(lo, hi, body):
        def one(r, _):
            body(r)
            return 0
        count = hi - lo
        step = next(u for u in (9, 8, 7, 6, 4, 3, 2, 1) if count % u == 0)
        lax.fori_loop(lo, hi, one, 0, unroll=step)

    def mid_one(p, lo, hi):
        def body(m):
            for (q, s), v in zip(halves, conv_row(x1, p, fw[0], m)):
                act, slope = gelu_both(v)
                act1[p, m, :, s] = act.astype(bf16)
                sl1[p, m, :, s] = slope.astype(bf16)
        loop(lo, hi, body)

    def second(p, lo, hi):
        def body(r):
            for (q, s), v in zip(halves, conv_row(act1, p, fw[1], r)):
                act, slope = gelu_both(v)
                act2[p + 1, r, :, s] = act.astype(bf16)
                sl2[p, r, :, s] = slope.astype(bf16)
        loop(lo, hi, body)

    def three(buf, first, r):
        early, late = buf[first, r], buf[first + 1, r]
        middle = jnp.concatenate([early[:, W:], late[:, :W]], axis=1)
        return early, middle, late

    def mix(p, lo, hi):
        def body(r):
            columns = jnp.concatenate(three(act2, p, r), axis=0)
            v = jnp.dot(tf[...], columns, preferred_element_type=f32)
            act, slope = gelu_both(v)
            x3[p, r + 2] = act.astype(bf16)
            sl3[p, r] = slope.astype(bf16)
        loop(lo, hi, body)

    def mid_four(p, lo, hi):
        def body(m):
            pre = conv_row(x3, p, fw[2], m)
            back = conv_row(xc, p, bw[3], m)
            for (q, s), v, g in zip(halves, pre, back):
                act, slope = gelu_both(v)
                act4[p, m, :, s] = act.astype(bf16)
                bk4[p, m, :, s] = (g * slope).astype(bf16)
        loop(lo, hi, body)

    def decode(p, lo, hi):
        def body(r):
            for (q, s), v in zip(halves, conv_row(act4, p, fw[3], r)):
                dec[p, r, :, s] = v.astype(bf16)
        loop(lo, hi, body)

    def back_three(p, lo, hi):
        def body(r):
            for (q, s), g in zip(halves, conv_row(bk4, p, bw[2], r)):
                b3[p, r, :, s] = (g * sl3[p, r, :, s].astype(f32)).astype(bf16)
        loop(lo, hi, body)

    def unmix(p, lo, hi):
        def body(r):
            columns = jnp.concatenate(three(b3, p, r), axis=0)
            g = jnp.dot(tb[...], columns, preferred_element_type=f32)
            x5[p, r + 2] = (g * sl2[p, r].astype(f32)).astype(bf16)
        loop(lo, hi, body)

    def back_one(p, lo, hi):
        def body(m):
            for (q, s), g in zip(halves, conv_row(x5, p, bw[1], m)):
                bk1[p, m, :, s] = (g * sl1[p, m, :, s].astype(f32)).astype(bf16)
        loop(lo, hi, body)

    def grads(p, lo, hi):
        def body(r):
            for (q, s), g in zip(halves, conv_row(bk1, p, bw[0], r)):
                grad[p, r, :, s] = g
        loop(lo, hi, body)

    def outside(p, bufs):
        @pl.when(jnp.logical_not(has_up))
        def _():
            for buf in bufs:
                buf[p, 0] = edge[0]

        @pl.when(jnp.logical_not(has_down))
        def _():
            for buf in bufs:
                buf[p, rows + 1] = edge[0]

    def store(which, f):
        src, dst = ((dec, dec_hbm), (grad, grad_hbm))[which]
        return pltpu.make_async_copy(
            src.at[f // 2, :, :, (f % 2) * W:(f % 2 + 1) * W], dst.at[f], out_sem.at[which, f])

    def stage_one(p):
        for f in (2 * p, 2 * p + 1):
            load(0, f).wait()
        mid_one(p, 2, rows)
        for f in (2 * p, 2 * p + 1):
            border_arrived(input_border(0, f))
        mid_one(p, 0, 2)
        mid_one(p, rows, rows + 2)
        outside(p, (act1, sl1))

    def start_pair(p):
        mid_four(p, 2, rows)
        border_arrived(pair_border(x3, x3s, x3r, p))
        mid_four(p, 0, 2)
        mid_four(p, rows, rows + 2)
        outside(p, (act4, bk4))

    stage_one(1)
    for i, (lo, hi) in enumerate(PIECES):
        second(1, lo, hi)
        when_start(has_next, a_piece(i))
    stage_one(0)
    second(0, 0, rows)
    for lo, hi in PIECES[:2]:
        mix(1, lo, hi)
    border_start(pair_border(x3, x3s, x3r, 1))
    mix(1, 2, rows - 2)
    for f in (2, 3):
        load(1, f).wait()
        border_arrived(input_border(1, f))
    start_pair(1)
    back_three(1, 0, rows)
    decode(1, 0, rows)
    for f in (2, 3):
        store(0, f).start()
    for f in (0, 1):
        load(1, f).wait()
        border_arrived(input_border(1, f))

    for i in (0, 1):
        when_recv(has_prev, a_piece(i))
        mix(0, *PIECES[i])
    border_start(pair_border(x3, x3s, x3r, 0))
    for i in (2, 3):
        when_recv(has_prev, a_piece(i))
        mix(0, *PIECES[i])
    start_pair(0)
    for i, (lo, hi) in enumerate(PIECES):
        back_three(0, lo, hi)
        when_start(has_prev, b_piece(i))
    for lo, hi in PIECES[:2]:
        unmix(0, lo, hi)
    border_start(pair_border(x5, x5s, x5r, 0))
    unmix(0, 2, rows - 2)
    decode(0, 0, rows)
    for f in (0, 1):
        store(0, f).start()
    border_arrived(pair_border(x5, x5s, x5r, 0))
    back_one(0, 0, rows + 2)
    grads(0, 0, rows)
    for f in (0, 1):
        store(1, f).start()

    for i in (0, 1):
        when_recv(has_next, b_piece(i))
        unmix(1, *PIECES[i])
    border_start(pair_border(x5, x5s, x5r, 1))
    for i in (2, 3):
        when_recv(has_next, b_piece(i))
        unmix(1, *PIECES[i])
    back_one(1, 2, rows)
    border_arrived(pair_border(x5, x5s, x5r, 1))
    back_one(1, 0, 2)
    back_one(1, rows, rows + 2)
    grads(1, 0, rows)
    for f in (2, 3):
        store(1, f).start()

    for which in range(2):
        for f in range(4):
            border_sent(input_border(which, f))
    for p in range(2):
        border_sent(pair_border(x3, x3s, x3r, p))
        border_sent(pair_border(x5, x5s, x5r, p))
    for i in range(len(PIECES)):
        when_sent(has_next, a_piece(i))
        when_sent(has_prev, b_piece(i))
    for which in range(2):
        for f in range(4):
            store(which, f).wait()


def per_device(sizes, frames_in, conv_one, conv_two, temporal, conv_three, conv_four, cotangent):
    frames, rows = frames_in.shape[:2]
    sizes = (*sizes, rows)
    taps = [jnp.transpose(k, (1, 2, 0, 3)) for k in (conv_one, conv_two, conv_three, conv_four)]
    bf16, f32 = jnp.bfloat16, jnp.float32

    def pair(extra, kind=bf16, count=2):
        return pltpu.VMEM((count, rows + extra, C, 2 * W), kind)

    dma = pltpu.SemaphoreType.DMA
    hbm = pl.BlockSpec(memory_space=pl.ANY)
    return pl.pallas_call(
        functools.partial(kernel, sizes),
        name="stack",
        out_shape=(jax.ShapeDtypeStruct(frames_in.shape, bf16), jax.ShapeDtypeStruct(frames_in.shape, f32)),
        in_specs=[hbm] * 7,
        out_specs=(hbm, hbm),
        scratch_shapes=[
            pair(4), pair(4), pair(4), pair(4),
            pair(2), pair(2),
            pair(0, count=3), pair(0), pair(0),
            pair(2), pair(2),
            pair(0, count=3),
            pair(2),
            pair(0), pair(0, f32),
            pltpu.VMEM((4, 3 * C, 3 * C), bf16), pltpu.VMEM((4, 3 * C, 3 * C), bf16),
            pltpu.VMEM((C, 3 * C), bf16), pltpu.VMEM((C, 3 * C), bf16),
            pltpu.VMEM((4, 3, 3, C, C), bf16), pltpu.VMEM((3, C, C), bf16),
            dma((5,)), dma((2, 4)), dma((2, 4)),
            dma((2, 4, 2)), dma((2, 4, 2)),
            dma((2, 2)), dma((2, 2)), dma((2, 2)), dma((2, 2)),
            dma((4,)), dma((4,)), dma((4,)), dma((4,)),
        ],
        compiler_params=pltpu.CompilerParams(collective_id=0, has_side_effects=True, vmem_limit_bytes=56 << 20),
    )(frames_in, taps[0], taps[1], temporal, taps[2], taps[3], cotangent)


def solution(mesh):
    split = P("tm", "rows", None, None)
    return jax.shard_map(
        functools.partial(per_device, (mesh.shape["tm"], mesh.shape["rows"])),
        mesh=mesh,
        in_specs=(split, P(), P(), P(), P(), P(), split),
        out_specs=(split, split),
        check_vma=False,
    )
```

```python
import functools

import jax
import jax.numpy as jnp
from jax import lax
from jax.experimental import pallas as pl
from jax.experimental.pallas import tpu as pltpu
from jax.sharding import PartitionSpec as P

SQRT_HALF = 0.7071067811865476
INV_ROOT_TAU = 0.3989422804014327
MESH = pl.DeviceIdType.MESH
C = 64
W = 128
PIECES = ((0, 2), (14, 16), (2, 8), (8, 14))
BACK_PIECES = ((0, 6), (14, 16), (6, 10), (10, 14))


def gelu_both(v):
    phi = 0.5 + 0.5 * lax.erf(v * SQRT_HALF)
    bump = jnp.exp(v * v * -0.5) * INV_ROOT_TAU
    return v * phi, phi + v * bump


def conv_row(window, weights):
    lane = lax.broadcasted_iota(jnp.int32, (C, W), 1)
    y = jnp.dot(weights, window.reshape(3 * C, 2 * W), preferred_element_type=jnp.float32)
    out = []
    for q in range(2):
        part = y[:, q * W:(q + 1) * W]
        left = jnp.where(lane == 0, 0.0, pltpu.roll(part[0:C], 1, 1))
        right = jnp.where(lane == W - 1, 0.0, pltpu.roll(part[2 * C:], W - 1, 1))
        out.append(left + part[C:2 * C] + right)
    return out


HALVES = (slice(0, W), slice(W, 2 * W))


def loop(lo, hi, body):
    def one(r, _):
        body(r)
        return 0
    lax.fori_loop(lo, hi, one, 0, unroll=hi - lo)


def last_kernel(rows, dec, grad0, bk1, bw1, dec_hbm, grad_hbm, grad1, sem):
    def store(which, f):
        src, dst = ((dec.at[f // 2], dec_hbm), ((grad0, grad1)[f // 2], grad_hbm))[which]
        return pltpu.make_async_copy(src.at[:, :, HALVES[f % 2]], dst.at[f], sem.at[which, f])

    for which, f in ((0, 0), (0, 1), (0, 2), (0, 3), (1, 0), (1, 1)):
        store(which, f).start()

    def body(r):
        for s, g in zip(HALVES, conv_row(bk1[pl.ds(r, 3)], bw1[...])):
            grad1[r, :, s] = g
    loop(0, rows, body)
    for f in (2, 3):
        store(1, f).start()
    for which in range(2):
        for f in range(4):
            store(which, f).wait()


def kernel(sizes, x_hbm, k1, k2, t_hbm, k3, k4, cot_hbm, dec, grad0, bk1_late, bw1,
           x1, xc, x3, x5, act1, sl1, act2, sl2, sl3, act4, bk4, b3, bk1_early, fw, bw, tf, tb, kraw, traw,
           w_sem, in_sem, hs, hr, x3s, x3r, x5s, x5r, a_s, a_r, b_s, b_r):
    n_tm, n_rows, rows = sizes
    tm = lax.axis_index("tm")
    band = lax.axis_index("rows")
    has_up, has_down = band > 0, band < n_rows - 1
    has_prev, has_next = tm > 0, tm < n_tm - 1
    bf16, f32 = jnp.bfloat16, jnp.float32

    w_copies = [pltpu.make_async_copy(k, kraw.at[i], w_sem.at[i]) for i, k in enumerate((k1, k2, k3, k4))]
    w_copies.append(pltpu.make_async_copy(t_hbm, traw, w_sem.at[4]))
    for c in w_copies:
        c.start()

    def load(which, f):
        src, dst = ((x_hbm, x1), (cot_hbm, xc))[which]
        return pltpu.make_async_copy(
            src.at[f], dst.at[f // 2, 2:rows + 2, :, (f % 2) * W:(f % 2 + 1) * W], in_sem.at[which, f])

    for which, f in ((0, 2), (0, 3), (0, 0), (0, 1), (1, 2), (1, 3), (1, 0), (1, 1)):
        load(which, f).start()

    barrier = pltpu.get_barrier_semaphore()
    count = jnp.int32(0)
    for ok, peer in ((has_up, {"rows": band - 1}), (has_down, {"rows": band + 1}),
                     (has_prev, {"tm": tm - 1}), (has_next, {"tm": tm + 1})):
        @pl.when(ok)
        def _():
            pl.semaphore_signal(barrier, inc=1, device_id=peer, device_id_type=MESH)
        count = count + ok.astype(jnp.int32)
    pl.semaphore_wait(barrier, count)

    def border(src_of, dst_of, send, recv, at):
        down = pltpu.make_async_remote_copy(
            src_of(rows - 2), dst_of(0), send.at[*at, 0], recv.at[*at, 0],
            device_id={"rows": band + 1}, device_id_type=MESH)
        up = pltpu.make_async_remote_copy(
            src_of(0), dst_of(rows + 2), send.at[*at, 1], recv.at[*at, 1],
            device_id={"rows": band - 1}, device_id_type=MESH)
        return down, up

    def border_start(copies):
        down, up = copies

        @pl.when(has_down)
        def _():
            down.start()

        @pl.when(has_up)
        def _():
            up.start()

    def border_arrived(copies):
        down, up = copies

        @pl.when(has_up)
        def _():
            down.wait_recv()

        @pl.when(has_down)
        def _():
            up.wait_recv()

    def border_sent(copies):
        down, up = copies

        @pl.when(has_down)
        def _():
            down.wait_send()

        @pl.when(has_up)
        def _():
            up.wait_send()

    def input_border(which, f):
        src, dst = ((x_hbm, x1), (cot_hbm, xc))[which]
        half = slice((f % 2) * W, (f % 2 + 1) * W)
        return border(lambda r: src.at[f, r:r + 2], lambda r: dst.at[f // 2, r:r + 2, :, half], hs, hr, (which, f))

    def pair_border(buf, send, recv, p):
        return border(lambda r: buf.at[p, r + 2:r + 4], lambda r: buf.at[p, r:r + 2], send, recv, (p,))

    for which, f in ((0, 2), (0, 3), (0, 0), (0, 1), (1, 2), (1, 3), (1, 0), (1, 1)):
        border_start(input_border(which, f))

    def a_piece(i):
        lo, hi = PIECES[i]
        return pltpu.make_async_remote_copy(
            act2.at[2, lo:hi], act2.at[0, lo:hi], a_s.at[i], a_r.at[i], device_id={"tm": tm + 1}, device_id_type=MESH)

    def b_piece(i):
        lo, hi = BACK_PIECES[i]
        return pltpu.make_async_remote_copy(
            b3.at[0, lo:hi], b3.at[2, lo:hi], b_s.at[i], b_r.at[i], device_id={"tm": tm - 1}, device_id_type=MESH)

    def when_start(ok, copy):
        @pl.when(ok)
        def _():
            copy.start()

    def when_recv(ok, copy):
        @pl.when(ok)
        def _():
            copy.wait_recv()

    def when_sent(ok, copy):
        @pl.when(ok)
        def _():
            copy.wait_send()

    edge = jnp.zeros((2, C, 2 * W), bf16)

    def clear_rows(bufs):
        @pl.when(jnp.logical_not(has_up))
        def _():
            for buf in bufs:
                for p in range(2):
                    buf[p, 0:2] = edge

        @pl.when(jnp.logical_not(has_down))
        def _():
            for buf in bufs:
                for p in range(2):
                    buf[p, rows + 2:rows + 4] = edge

    def clear(ref, at):
        def one(r, _):
            ref[at, r] = edge[0]
            return 0
        lax.fori_loop(0, rows, one, 0)

    def clear_frames():
        @pl.when(jnp.logical_not(has_prev))
        def _():
            clear(act2, 0)

        @pl.when(jnp.logical_not(has_next))
        def _():
            clear(b3, 2)

    def arrange(n):
        for b in range(3):
            fw[n, b * C:(b + 1) * C, :] = jnp.concatenate(
                [kraw[n, a, b].astype(f32) for a in range(3)], axis=1).astype(bf16)

    def arrange_back(n):
        ref = bw1 if n == 0 else bw.at[n - 1]
        for b in range(3):
            ref[b * C:(b + 1) * C, :] = jnp.concatenate(
                [kraw[n, 2 - a, 2 - b].astype(f32).T for a in range(3)], axis=1).astype(bf16)

    def arrange_lags():
        lags = [traw[j].astype(f32) for j in range(3)]
        tf[...] = jnp.concatenate(lags, axis=1).astype(bf16)
        tb[...] = jnp.concatenate([k.T for k in lags[::-1]], axis=1).astype(bf16)

    def mid_one(p, lo, hi):
        def body(m):
            for s, v in zip(HALVES, conv_row(x1[p, pl.ds(m, 3)], fw[0])):
                act, slope = gelu_both(v)
                act1[p, m, :, s] = act.astype(bf16)
                sl1[p, m, :, s] = slope.astype(bf16)
        loop(lo, hi, body)

    def second(p, lo, hi):
        def body(r):
            for s, v in zip(HALVES, conv_row(act1[p, pl.ds(r, 3)], fw[1])):
                act, slope = gelu_both(v)
                act2[p + 1, r, :, s] = act.astype(bf16)
                sl2[p, r, :, s] = slope.astype(bf16)
        loop(lo, hi, body)

    def three(buf, first, r):
        early, late = buf[first, r], buf[first + 1, r]
        middle = jnp.concatenate([early[:, W:], late[:, :W]], axis=1)
        return early, middle, late

    def mix(p, lo, hi):
        def body(r):
            columns = jnp.concatenate(three(act2, p, r), axis=0)
            v = jnp.dot(tf[...], columns, preferred_element_type=f32)
            act, slope = gelu_both(v)
            x3[p, r + 2] = act.astype(bf16)
            sl3[p, r] = slope.astype(bf16)
        loop(lo, hi, body)

    def mid_four(p, lo, hi):
        def body(m):
            pre = conv_row(x3[p, pl.ds(m, 3)], fw[2])
            back = conv_row(xc[p, pl.ds(m, 3)], bw[2])
            for s, v, g in zip(HALVES, pre, back):
                act, slope = gelu_both(v)
                act4[p, m, :, s] = act.astype(bf16)
                bk4[p, m, :, s] = (g * slope).astype(bf16)
        loop(lo, hi, body)

    def decode(p, lo, hi):
        def body(r):
            for s, v in zip(HALVES, conv_row(act4[p, pl.ds(r, 3)], fw[3])):
                dec[p, r, :, s] = v.astype(bf16)
        loop(lo, hi, body)

    def back_three(p, lo, hi):
        def body(r):
            for s, g in zip(HALVES, conv_row(bk4[p, pl.ds(r, 3)], bw[1])):
                b3[p, r, :, s] = (g * sl3[p, r, :, s].astype(f32)).astype(bf16)
        loop(lo, hi, body)

    def unmix(p, lo, hi):
        def body(r):
            columns = jnp.concatenate(three(b3, p, r), axis=0)
            g = jnp.dot(tb[...], columns, preferred_element_type=f32)
            x5[p, r + 2] = (g * sl2[p, r].astype(f32)).astype(bf16)
        loop(lo, hi, body)

    def back_one(p, lo, hi):
        bk1 = (bk1_early, bk1_late)[p]

        def body(m):
            for s, g in zip(HALVES, conv_row(x5[p, pl.ds(m, 3)], bw[0])):
                bk1[m, :, s] = (g * sl1[p, m, :, s].astype(f32)).astype(bf16)
        loop(lo, hi, body)

    def grads(lo, hi):
        def body(r):
            for s, g in zip(HALVES, conv_row(bk1_early[pl.ds(r, 3)], bw1[...])):
                grad0[r, :, s] = g
        loop(lo, hi, body)

    def outside_first(p, bufs):
        @pl.when(jnp.logical_not(has_up))
        def _():
            for buf in bufs:
                buf[p, 0] = edge[0]

    def outside_last(p, bufs):
        @pl.when(jnp.logical_not(has_down))
        def _():
            for buf in bufs:
                buf[p, rows + 1] = edge[0]

    def outside(p, bufs):
        outside_first(p, bufs)
        outside_last(p, bufs)

    def stage_one(p):
        for f in (2 * p, 2 * p + 1):
            load(0, f).wait()
        mid_one(p, 2, rows)
        for f in (2 * p, 2 * p + 1):
            border_arrived(input_border(0, f))
        mid_one(p, 0, 2)
        mid_one(p, rows, rows + 2)
        outside(p, (act1, sl1))

    w_copies[0].wait()
    arrange(0)
    clear_rows((x1,))
    stage_one(1)
    w_copies[1].wait()
    arrange(1)
    for i, (lo, hi) in enumerate(PIECES):
        second(1, lo, hi)
        when_start(has_next, a_piece(i))
    stage_one(0)
    second(0, 0, rows)
    clear_rows((xc, x3, x5))
    for i in (2, 3, 4):
        w_copies[i].wait()
    arrange_lags()
    for lo, hi in PIECES[:2]:
        mix(1, lo, hi)
    border_start(pair_border(x3, x3s, x3r, 1))
    mix(1, 2, rows - 2)
    arrange(2)
    arrange_back(3)
    for f in (2, 3):
        load(1, f).wait()
        border_arrived(input_border(1, f))
    mid_four(1, 2, rows)
    border_arrived(pair_border(x3, x3s, x3r, 1))
    mid_four(1, 0, 2)
    mid_four(1, rows, rows + 2)
    outside(1, (act4, bk4))
    arrange_back(2)
    back_three(1, 0, rows)
    arrange(3)
    decode(1, 0, rows)
    arrange_back(1)
    arrange_back(0)
    clear_frames()
    for f in (0, 1):
        load(1, f).wait()
        border_arrived(input_border(1, f))

    for i in (0, 1):
        when_recv(has_prev, a_piece(i))
        mix(0, *PIECES[i])
    border_start(pair_border(x3, x3s, x3r, 0))
    when_recv(has_prev, a_piece(2))
    mix(0, *PIECES[2])
    border_arrived(pair_border(x3, x3s, x3r, 0))
    mid_four(0, 0, 8)
    outside_first(0, (act4, bk4))
    back_three(0, *BACK_PIECES[0])
    when_start(has_prev, b_piece(0))
    when_recv(has_prev, a_piece(3))
    mix(0, *PIECES[3])
    mid_four(0, 8, rows + 2)
    outside_last(0, (act4, bk4))
    for i in (1, 2, 3):
        back_three(0, *BACK_PIECES[i])
        when_start(has_prev, b_piece(i))
    unmix(0, 0, 2)
    unmix(0, rows - 2, rows)
    border_start(pair_border(x5, x5s, x5r, 0))
    unmix(0, 2, rows - 2)
    decode(0, 0, rows)
    border_arrived(pair_border(x5, x5s, x5r, 0))
    back_one(0, 0, rows + 2)
    grads(0, rows)

    for i in (0, 1):
        when_recv(has_next, b_piece(i))
        unmix(1, *BACK_PIECES[i])
    border_start(pair_border(x5, x5s, x5r, 1))
    when_recv(has_next, b_piece(2))
    unmix(1, *BACK_PIECES[2])
    border_arrived(pair_border(x5, x5s, x5r, 1))
    back_one(1, 0, 10)
    when_recv(has_next, b_piece(3))
    unmix(1, *BACK_PIECES[3])
    back_one(1, 10, rows + 2)

    for which in range(2):
        for f in range(4):
            border_sent(input_border(which, f))
    for p in range(2):
        border_sent(pair_border(x3, x3s, x3r, p))
        border_sent(pair_border(x5, x5s, x5r, p))
    for i in range(len(PIECES)):
        when_sent(has_next, a_piece(i))
        when_sent(has_prev, b_piece(i))


def per_device(sizes, frames_in, conv_one, conv_two, temporal, conv_three, conv_four, cotangent):
    frames, rows = frames_in.shape[:2]
    sizes = (*sizes, rows)
    taps = [jnp.transpose(k, (1, 2, 0, 3)) for k in (conv_one, conv_two, conv_three, conv_four)]
    bf16, f32 = jnp.bfloat16, jnp.float32

    def pair(extra, count=2):
        return pltpu.VMEM((count, rows + extra, C, 2 * W), bf16)

    dma = pltpu.SemaphoreType.DMA
    hbm, vmem = pl.BlockSpec(memory_space=pltpu.HBM), pl.BlockSpec(memory_space=pltpu.VMEM)
    matrix = (3 * C, 3 * C)
    halfway = pl.pallas_call(
        functools.partial(kernel, sizes),
        name="stack",
        out_shape=(
            jax.ShapeDtypeStruct((2, rows, C, 2 * W), bf16),
            jax.ShapeDtypeStruct((rows, C, 2 * W), f32),
            jax.ShapeDtypeStruct((rows + 2, C, 2 * W), bf16),
            jax.ShapeDtypeStruct(matrix, bf16),
        ),
        in_specs=[hbm] * 7,
        out_specs=(vmem,) * 4,
        scratch_shapes=[
            pair(4), pair(4), pair(4), pair(4),
            pair(2), pair(2),
            pair(0, count=3), pair(0), pair(0),
            pair(2), pair(2),
            pair(0, count=3),
            pltpu.VMEM((rows + 2, C, 2 * W), bf16),
            pltpu.VMEM((4, *matrix), bf16), pltpu.VMEM((3, *matrix), bf16),
            pltpu.VMEM((C, 3 * C), bf16), pltpu.VMEM((C, 3 * C), bf16),
            pltpu.VMEM((4, 3, 3, C, C), bf16), pltpu.VMEM((3, C, C), bf16),
            dma((5,)), dma((2, 4)),
            dma((2, 4, 2)), dma((2, 4, 2)),
            dma((2, 2)), dma((2, 2)), dma((2, 2)), dma((2, 2)),
            dma((4,)), dma((4,)), dma((4,)), dma((4,)),
        ],
        compiler_params=pltpu.CompilerParams(collective_id=0, has_side_effects=True, vmem_limit_bytes=36 << 20),
    )(*[pltpu.with_memory_space_constraint(v, pltpu.HBM) for v in (frames_in, taps[0], taps[1], temporal, taps[2], taps[3], cotangent)])
    return pl.pallas_call(
        functools.partial(last_kernel, rows),
        name="last",
        out_shape=(jax.ShapeDtypeStruct(frames_in.shape, bf16), jax.ShapeDtypeStruct(frames_in.shape, f32)),
        in_specs=[vmem] * 4,
        out_specs=(hbm, hbm),
        scratch_shapes=[pltpu.VMEM((rows, C, 2 * W), f32), dma((2, 4))],
        compiler_params=pltpu.CompilerParams(vmem_limit_bytes=16 << 20),
    )(*halfway)


def solution(mesh):
    split = P("tm", "rows", None, None)
    return jax.shard_map(
        functools.partial(per_device, (mesh.shape["tm"], mesh.shape["rows"])),
        mesh=mesh,
        in_specs=(split, P(), P(), P(), P(), P(), split),
        out_specs=(split, split),
        check_vma=False,
    )
```

```python
import functools

import jax
import jax.numpy as jnp
from jax import lax
from jax.experimental import pallas as pl
from jax.experimental.pallas import tpu as pltpu
from jax.sharding import PartitionSpec as P

SQRT_HALF = 0.7071067811865476
INV_ROOT_TAU = 0.3989422804014327
MESH = pl.DeviceIdType.MESH
C = 64
W = 128
PIECES = ((2, 6), (0, 2), (14, 16), (6, 10), (10, 14))
BACK_PIECES = ((0, 4), (4, 8), (14, 16), (8, 11), (11, 14))


def gelu_both(v):
    phi = 0.5 + 0.5 * lax.erf(v * SQRT_HALF)
    bump = jnp.exp(v * v * -0.5) * INV_ROOT_TAU
    return v * phi, phi + v * bump


def conv_row(window, weights):
    lane = lax.broadcasted_iota(jnp.int32, (C, W), 1)
    y = jnp.dot(weights, window.reshape(3 * C, 2 * W), preferred_element_type=jnp.float32)
    out = []
    for q in range(2):
        part = y[:, q * W:(q + 1) * W]
        left = jnp.where(lane == 0, 0.0, pltpu.roll(part[0:C], 1, 1))
        right = jnp.where(lane == W - 1, 0.0, pltpu.roll(part[2 * C:], W - 1, 1))
        out.append(left + part[C:2 * C] + right)
    return out


HALVES = (slice(0, W), slice(W, 2 * W))


def loop(lo, hi, body):
    def one(r, _):
        body(r)
        return 0
    lax.fori_loop(lo, hi, one, 0, unroll=hi - lo)


def last_kernel(rows, dec, grad0, bk1, bw1, dec_hbm, grad_hbm, grad1, sem):
    def store(which, f):
        src, dst = ((dec.at[f // 2], dec_hbm), ((grad0, grad1)[f // 2], grad_hbm))[which]
        return pltpu.make_async_copy(src.at[:, :, HALVES[f % 2]], dst.at[f], sem.at[which, f])

    for which, f in ((0, 0), (0, 1), (0, 2), (0, 3), (1, 0), (1, 1)):
        store(which, f).start()

    def body(r):
        for s, g in zip(HALVES, conv_row(bk1[pl.ds(r, 3)], bw1[...])):
            grad1[r, :, s] = g
    loop(0, rows, body)
    for f in (2, 3):
        store(1, f).start()
    for which in range(2):
        for f in range(4):
            store(which, f).wait()


def kernel(sizes, x_hbm, k1, k2, t_hbm, k3, k4, cot_hbm, dec, grad0, bk1_late, bw1,
           x1, xc, x3, x5, act1, sl1, act2, sl2, sl3, act4, bk4, g4, b3, bk1_early, fw, bw, tf, tb, kraw, traw,
           w_sem, in_sem, hs, hr, x3s, x3r, x5s, x5r, a_s, a_r, b_s, b_r):
    n_tm, n_rows, rows = sizes
    tm = lax.axis_index("tm")
    band = lax.axis_index("rows")
    has_up, has_down = band > 0, band < n_rows - 1
    has_prev, has_next = tm > 0, tm < n_tm - 1
    bf16, f32 = jnp.bfloat16, jnp.float32

    w_copies = [pltpu.make_async_copy(k, kraw.at[i], w_sem.at[i]) for i, k in enumerate((k1, k2, k3, k4))]
    w_copies.append(pltpu.make_async_copy(t_hbm, traw, w_sem.at[4]))
    for c in w_copies:
        c.start()

    def load(which, f):
        src, dst = ((x_hbm, x1), (cot_hbm, xc))[which]
        return pltpu.make_async_copy(
            src.at[f], dst.at[f // 2, 2:rows + 2, :, (f % 2) * W:(f % 2 + 1) * W], in_sem.at[which, f])

    for which, f in ((0, 2), (0, 3), (0, 0), (0, 1), (1, 2), (1, 3), (1, 0), (1, 1)):
        load(which, f).start()

    barrier = pltpu.get_barrier_semaphore()
    count = jnp.int32(0)
    for ok, peer in ((has_up, {"rows": band - 1}), (has_down, {"rows": band + 1}),
                     (has_prev, {"tm": tm - 1}), (has_next, {"tm": tm + 1})):
        @pl.when(ok)
        def _():
            pl.semaphore_signal(barrier, inc=1, device_id=peer, device_id_type=MESH)
        count = count + ok.astype(jnp.int32)
    pl.semaphore_wait(barrier, count)

    def border(src_of, dst_of, send, recv, at):
        down = pltpu.make_async_remote_copy(
            src_of(rows - 2), dst_of(0), send.at[*at, 0], recv.at[*at, 0],
            device_id={"rows": band + 1}, device_id_type=MESH)
        up = pltpu.make_async_remote_copy(
            src_of(0), dst_of(rows + 2), send.at[*at, 1], recv.at[*at, 1],
            device_id={"rows": band - 1}, device_id_type=MESH)
        return down, up

    def border_start(copies):
        down, up = copies

        @pl.when(has_down)
        def _():
            down.start()

        @pl.when(has_up)
        def _():
            up.start()

    def border_arrived(copies):
        down, up = copies

        @pl.when(has_up)
        def _():
            down.wait_recv()

        @pl.when(has_down)
        def _():
            up.wait_recv()

    def border_sent(copies):
        down, up = copies

        @pl.when(has_down)
        def _():
            down.wait_send()

        @pl.when(has_up)
        def _():
            up.wait_send()

    def input_border(which, f):
        src, dst = ((x_hbm, x1), (cot_hbm, xc))[which]
        half = slice((f % 2) * W, (f % 2 + 1) * W)
        return border(lambda r: src.at[f, r:r + 2], lambda r: dst.at[f // 2, r:r + 2, :, half], hs, hr, (which, f))

    def pair_border(buf, send, recv, p):
        return border(lambda r: buf.at[p, r + 2:r + 4], lambda r: buf.at[p, r:r + 2], send, recv, (p,))

    for which, f in ((0, 2), (0, 3), (0, 0), (0, 1), (1, 2), (1, 3), (1, 0), (1, 1)):
        border_start(input_border(which, f))

    def a_piece(i):
        lo, hi = PIECES[i]
        return pltpu.make_async_remote_copy(
            act2.at[2, lo:hi], act2.at[0, lo:hi], a_s.at[i], a_r.at[i], device_id={"tm": tm + 1}, device_id_type=MESH)

    def b_piece(i):
        lo, hi = BACK_PIECES[i]
        return pltpu.make_async_remote_copy(
            b3.at[0, lo:hi], b3.at[2, lo:hi], b_s.at[i], b_r.at[i], device_id={"tm": tm - 1}, device_id_type=MESH)

    def when_start(ok, copy):
        @pl.when(ok)
        def _():
            copy.start()

    def when_recv(ok, copy):
        @pl.when(ok)
        def _():
            copy.wait_recv()

    def when_sent(ok, copy):
        @pl.when(ok)
        def _():
            copy.wait_send()

    edge = jnp.zeros((2, C, 2 * W), bf16)

    def clear_rows(bufs):
        @pl.when(jnp.logical_not(has_up))
        def _():
            for buf in bufs:
                for p in range(2):
                    buf[p, 0:2] = edge

        @pl.when(jnp.logical_not(has_down))
        def _():
            for buf in bufs:
                for p in range(2):
                    buf[p, rows + 2:rows + 4] = edge

    def clear(ref, at):
        def one(r, _):
            ref[at, r] = edge[0]
            return 0
        lax.fori_loop(0, rows, one, 0)

    def clear_frames():
        @pl.when(jnp.logical_not(has_prev))
        def _():
            clear(act2, 0)

        @pl.when(jnp.logical_not(has_next))
        def _():
            clear(b3, 2)

    def arrange(n):
        for b in range(3):
            fw[n, b * C:(b + 1) * C, :] = jnp.concatenate(
                [kraw[n, a, b].astype(f32) for a in range(3)], axis=1).astype(bf16)

    def arrange_back(n):
        ref = bw1 if n == 0 else bw.at[n - 1]
        for b in range(3):
            ref[b * C:(b + 1) * C, :] = jnp.concatenate(
                [kraw[n, 2 - a, 2 - b].astype(f32).T for a in range(3)], axis=1).astype(bf16)

    def arrange_lags():
        lags = [traw[j].astype(f32) for j in range(3)]
        tf[...] = jnp.concatenate(lags, axis=1).astype(bf16)
        tb[...] = jnp.concatenate([k.T for k in lags[::-1]], axis=1).astype(bf16)

    def mid_one(p, lo, hi):
        def body(m):
            for s, v in zip(HALVES, conv_row(x1[p, pl.ds(m, 3)], fw[0])):
                act, slope = gelu_both(v)
                act1[p, m, :, s] = act.astype(bf16)
                sl1[p, m, :, s] = slope.astype(bf16)
        loop(lo, hi, body)

    def second(p, lo, hi):
        def body(r):
            for s, v in zip(HALVES, conv_row(act1[p, pl.ds(r, 3)], fw[1])):
                act, slope = gelu_both(v)
                act2[p + 1, r, :, s] = act.astype(bf16)
                sl2[p, r, :, s] = slope.astype(bf16)
        loop(lo, hi, body)

    def three(buf, first, r):
        early, late = buf[first, r], buf[first + 1, r]
        middle = jnp.concatenate([early[:, W:], late[:, :W]], axis=1)
        return early, middle, late

    def mix(p, lo, hi):
        def body(r):
            columns = jnp.concatenate(three(act2, p, r), axis=0)
            v = jnp.dot(tf[...], columns, preferred_element_type=f32)
            act, slope = gelu_both(v)
            x3[p, r + 2] = act.astype(bf16)
            sl3[p, r] = slope.astype(bf16)
        loop(lo, hi, body)

    def mid_four(p, lo, hi):
        def body(m):
            pre = conv_row(x3[p, pl.ds(m, 3)], fw[2])
            back = conv_row(xc[p, pl.ds(m, 3)], bw[2]) if p else [g4[m, :, s] for s in HALVES]
            for s, v, g in zip(HALVES, pre, back):
                act, slope = gelu_both(v)
                act4[p, m, :, s] = act.astype(bf16)
                bk4[p, m, :, s] = (g * slope).astype(bf16)
        loop(lo, hi, body)

    def back_cotangent(lo, hi):
        def body(m):
            for s, g in zip(HALVES, conv_row(xc[0, pl.ds(m, 3)], bw[2])):
                g4[m, :, s] = g
        loop(lo, hi, body)

    def decode(p, lo, hi):
        def body(r):
            for s, v in zip(HALVES, conv_row(act4[p, pl.ds(r, 3)], fw[3])):
                dec[p, r, :, s] = v.astype(bf16)
        loop(lo, hi, body)

    def back_three(p, lo, hi):
        def body(r):
            for s, g in zip(HALVES, conv_row(bk4[p, pl.ds(r, 3)], bw[1])):
                b3[p, r, :, s] = (g * sl3[p, r, :, s].astype(f32)).astype(bf16)
        loop(lo, hi, body)

    def unmix(p, lo, hi):
        def body(r):
            columns = jnp.concatenate(three(b3, p, r), axis=0)
            g = jnp.dot(tb[...], columns, preferred_element_type=f32)
            x5[p, r + 2] = (g * sl2[p, r].astype(f32)).astype(bf16)
        loop(lo, hi, body)

    def back_one(p, lo, hi):
        bk1 = (bk1_early, bk1_late)[p]

        def body(m):
            for s, g in zip(HALVES, conv_row(x5[p, pl.ds(m, 3)], bw[0])):
                bk1[m, :, s] = (g * sl1[p, m, :, s].astype(f32)).astype(bf16)
        loop(lo, hi, body)

    def grads(lo, hi):
        def body(r):
            for s, g in zip(HALVES, conv_row(bk1_early[pl.ds(r, 3)], bw1[...])):
                grad0[r, :, s] = g
        loop(lo, hi, body)

    def outside_first(p, bufs):
        @pl.when(jnp.logical_not(has_up))
        def _():
            for buf in bufs:
                buf[p, 0] = edge[0]

    def outside_last(p, bufs):
        @pl.when(jnp.logical_not(has_down))
        def _():
            for buf in bufs:
                buf[p, rows + 1] = edge[0]

    def outside(p, bufs):
        outside_first(p, bufs)
        outside_last(p, bufs)

    def edges(step, p, extra=0):
        step(p, 0, 2)
        step(p, rows - 2 + extra, rows + extra)

    def input_arrived(which, p):
        for f in (2 * p, 2 * p + 1):
            border_arrived(input_border(which, f))

    w_copies[0].wait()
    arrange(0)
    for f in (2, 3):
        load(0, f).wait()
    mid_one(1, 2, rows)
    w_copies[1].wait()
    arrange(1)
    second(1, 2, 6)
    when_start(has_next, a_piece(0))
    second(1, 6, rows - 2)
    for f in (0, 1):
        load(0, f).wait()
    mid_one(0, 2, rows)
    second(0, 2, rows - 2)
    clear_rows((x1,))
    input_arrived(0, 1)
    edges(mid_one, 1, 2)
    outside(1, (act1, sl1))
    edges(second, 1)
    for i in range(1, len(PIECES)):
        when_start(has_next, a_piece(i))
    input_arrived(0, 0)
    edges(mid_one, 0, 2)
    outside(0, (act1, sl1))
    edges(second, 0)
    for i in (2, 3, 4):
        w_copies[i].wait()
    arrange_lags()
    edges(mix, 1)
    border_start(pair_border(x3, x3s, x3r, 1))
    mix(1, 2, rows - 2)

    clear_rows((xc, x3, x5))
    for f in (2, 3, 0, 1):
        load(1, f).wait()
        border_arrived(input_border(1, f))
    arrange(2)
    arrange_back(3)
    mid_four(1, 2, rows)
    arrange_back(2)
    back_three(1, 2, rows - 2)
    back_cotangent(0, rows + 2)
    arrange(3)
    decode(1, 2, rows - 2)
    arrange_back(1)
    arrange_back(0)
    clear_frames()
    border_arrived(pair_border(x3, x3s, x3r, 1))
    edges(mid_four, 1, 2)
    outside(1, (act4, bk4))
    edges(back_three, 1)
    edges(decode, 1)

    for i in (0, 1, 2):
        when_recv(has_prev, a_piece(i))
        mix(0, *PIECES[i])
    border_start(pair_border(x3, x3s, x3r, 0))
    when_recv(has_prev, a_piece(3))
    mix(0, *PIECES[3])
    mid_four(0, 2, 10)
    border_arrived(pair_border(x3, x3s, x3r, 0))
    mid_four(0, 0, 2)
    outside_first(0, (act4, bk4))
    for i in (0, 1):
        back_three(0, *BACK_PIECES[i])
        when_start(has_prev, b_piece(i))
    when_recv(has_prev, a_piece(4))
    mix(0, *PIECES[4])
    mid_four(0, 10, rows + 2)
    outside_last(0, (act4, bk4))
    for i in (2, 3, 4):
        back_three(0, *BACK_PIECES[i])
        when_start(has_prev, b_piece(i))
    edges(unmix, 0)
    border_start(pair_border(x5, x5s, x5r, 0))
    unmix(0, 2, rows - 2)
    decode(0, 0, rows)
    back_one(0, 2, rows)
    grads(2, rows - 2)
    border_arrived(pair_border(x5, x5s, x5r, 0))
    edges(back_one, 0, 2)
    grads(0, 2)
    grads(rows - 2, rows)

    for i in (0, 1, 2):
        when_recv(has_next, b_piece(i))
        unmix(1, *BACK_PIECES[i])
    border_start(pair_border(x5, x5s, x5r, 1))
    when_recv(has_next, b_piece(3))
    unmix(1, *BACK_PIECES[3])
    back_one(1, 2, 11)
    when_recv(has_next, b_piece(4))
    unmix(1, *BACK_PIECES[4])
    back_one(1, 11, rows)
    border_arrived(pair_border(x5, x5s, x5r, 1))
    edges(back_one, 1, 2)

    for which in range(2):
        for f in range(4):
            border_sent(input_border(which, f))
    for p in range(2):
        border_sent(pair_border(x3, x3s, x3r, p))
        border_sent(pair_border(x5, x5s, x5r, p))
    for i in range(len(PIECES)):
        when_sent(has_next, a_piece(i))
        when_sent(has_prev, b_piece(i))


def per_device(sizes, frames_in, conv_one, conv_two, temporal, conv_three, conv_four, cotangent):
    frames, rows = frames_in.shape[:2]
    sizes = (*sizes, rows)
    taps = [jnp.transpose(k, (1, 2, 0, 3)) for k in (conv_one, conv_two, conv_three, conv_four)]
    bf16, f32 = jnp.bfloat16, jnp.float32

    def pair(extra, count=2):
        return pltpu.VMEM((count, rows + extra, C, 2 * W), bf16)

    dma = pltpu.SemaphoreType.DMA
    hbm, vmem = pl.BlockSpec(memory_space=pltpu.HBM), pl.BlockSpec(memory_space=pltpu.VMEM)
    matrix = (3 * C, 3 * C)
    halfway = pl.pallas_call(
        functools.partial(kernel, sizes),
        name="stack",
        out_shape=(
            jax.ShapeDtypeStruct((2, rows, C, 2 * W), bf16),
            jax.ShapeDtypeStruct((rows, C, 2 * W), f32),
            jax.ShapeDtypeStruct((rows + 2, C, 2 * W), bf16),
            jax.ShapeDtypeStruct(matrix, bf16),
        ),
        in_specs=[hbm] * 7,
        out_specs=(vmem,) * 4,
        scratch_shapes=[
            pair(4), pair(4), pair(4), pair(4),
            pair(2), pair(2),
            pair(0, count=3), pair(0), pair(0),
            pair(2), pair(2), pltpu.VMEM((rows + 2, C, 2 * W), f32),
            pair(0, count=3),
            pltpu.VMEM((rows + 2, C, 2 * W), bf16),
            pltpu.VMEM((4, *matrix), bf16), pltpu.VMEM((3, *matrix), bf16),
            pltpu.VMEM((C, 3 * C), bf16), pltpu.VMEM((C, 3 * C), bf16),
            pltpu.VMEM((4, 3, 3, C, C), bf16), pltpu.VMEM((3, C, C), bf16),
            dma((5,)), dma((2, 4)),
            dma((2, 4, 2)), dma((2, 4, 2)),
            dma((2, 2)), dma((2, 2)), dma((2, 2)), dma((2, 2)),
            dma((5,)), dma((5,)), dma((5,)), dma((5,)),
        ],
        compiler_params=pltpu.CompilerParams(collective_id=0, has_side_effects=True, vmem_limit_bytes=36 << 20),
    )(*[pltpu.with_memory_space_constraint(v, pltpu.HBM) for v in (frames_in, taps[0], taps[1], temporal, taps[2], taps[3], cotangent)])
    return pl.pallas_call(
        functools.partial(last_kernel, rows),
        name="last",
        out_shape=(jax.ShapeDtypeStruct(frames_in.shape, bf16), jax.ShapeDtypeStruct(frames_in.shape, f32)),
        in_specs=[vmem] * 4,
        out_specs=(hbm, hbm),
        scratch_shapes=[pltpu.VMEM((rows, C, 2 * W), f32), dma((2, 4))],
        compiler_params=pltpu.CompilerParams(vmem_limit_bytes=16 << 20),
    )(*halfway)


def solution(mesh):
    split = P("tm", "rows", None, None)
    return jax.shard_map(
        functools.partial(per_device, (mesh.shape["tm"], mesh.shape["rows"])),
        mesh=mesh,
        in_specs=(split, P(), P(), P(), P(), P(), split),
        out_specs=(split, split),
        check_vma=False,
    )
```

```python
import functools

import jax
import jax.numpy as jnp
from jax import lax
from jax.experimental import pallas as pl
from jax.experimental.pallas import tpu as pltpu
from jax.sharding import PartitionSpec as P

SQRT_HALF = 0.7071067811865476
INV_ROOT_TAU = 0.3989422804014327
MESH = pl.DeviceIdType.MESH
C = 64
W = 128
PIECES = ((2, 6), (0, 2), (14, 16), (6, 10), (10, 14))
BACK_PIECES = ((0, 4), (4, 8), (14, 16), (8, 11), (11, 14))


def gelu_both(v):
    phi = 0.5 + 0.5 * lax.erf(v * SQRT_HALF)
    bump = jnp.exp(v * v * -0.5) * INV_ROOT_TAU
    return v * phi, phi + v * bump


def conv_row(window, weights):
    lane = lax.broadcasted_iota(jnp.int32, (C, W), 1)
    y = jnp.dot(weights, window.reshape(3 * C, 2 * W), preferred_element_type=jnp.float32)
    out = []
    for q in range(2):
        part = y[:, q * W:(q + 1) * W]
        left = jnp.where(lane == 0, 0.0, pltpu.roll(part[0:C], 1, 1))
        right = jnp.where(lane == W - 1, 0.0, pltpu.roll(part[2 * C:], W - 1, 1))
        out.append(left + part[C:2 * C] + right)
    return out


HALVES = (slice(0, W), slice(W, 2 * W))


def loop(lo, hi, body):
    def one(r, _):
        body(r)
        return 0
    lax.fori_loop(lo, hi, one, 0, unroll=hi - lo)


def last_kernel(rows, dec, grad0, bk1, bw1, dec_hbm, grad_hbm, grad1, sem):
    def store(which, f):
        src, dst = ((dec.at[f // 2], dec_hbm), ((grad0, grad1)[f // 2], grad_hbm))[which]
        return pltpu.make_async_copy(src.at[:, :, HALVES[f % 2]], dst.at[f], sem.at[which, f])

    for which, f in ((0, 0), (0, 1), (0, 2), (0, 3), (1, 0), (1, 1)):
        store(which, f).start()

    def body(r):
        for s, g in zip(HALVES, conv_row(bk1[pl.ds(r, 3)], bw1[...])):
            grad1[r, :, s] = g
    loop(0, rows, body)
    for f in (2, 3):
        store(1, f).start()
    for which in range(2):
        for f in range(4):
            store(which, f).wait()


def kernel(sizes, x_hbm, k1, k2, t_hbm, k3, k4, cot_hbm, dec, grad0, bk1_late, bw1,
           x1, xc, x3, x5, act1, sl1, act2, sl2, sl3, act4, bk4, g4, b3, bk1_early, fw, bw, tf, tb, kraw, traw,
           w_sem, in_sem, hs, hr, x3s, x3r, x5s, x5r, a_s, a_r, b_s, b_r):
    n_tm, n_rows, rows = sizes
    tm = lax.axis_index("tm")
    band = lax.axis_index("rows")
    has_up, has_down = band > 0, band < n_rows - 1
    has_prev, has_next = tm > 0, tm < n_tm - 1
    bf16, f32 = jnp.bfloat16, jnp.float32

    w_copies = [pltpu.make_async_copy(k, kraw.at[i], w_sem.at[i]) for i, k in enumerate((k1, k2, k3, k4))]
    w_copies.append(pltpu.make_async_copy(t_hbm, traw, w_sem.at[4]))
    for c in w_copies:
        c.start()

    def load(which, f):
        src, dst = ((x_hbm, x1), (cot_hbm, xc))[which]
        return pltpu.make_async_copy(
            src.at[f], dst.at[f // 2, 2:rows + 2, :, (f % 2) * W:(f % 2 + 1) * W], in_sem.at[which, f])

    for which, f in ((0, 2), (0, 3), (0, 0), (0, 1), (1, 2), (1, 3), (1, 0), (1, 1)):
        load(which, f).start()

    barrier = pltpu.get_barrier_semaphore()
    count = jnp.int32(0)
    for ok, peer in ((has_up, {"rows": band - 1}), (has_down, {"rows": band + 1}),
                     (has_prev, {"tm": tm - 1}), (has_next, {"tm": tm + 1})):
        @pl.when(ok)
        def _():
            pl.semaphore_signal(barrier, inc=1, device_id=peer, device_id_type=MESH)
        count = count + ok.astype(jnp.int32)
    pl.semaphore_wait(barrier, count)

    def border(src_of, dst_of, send, recv, at):
        down = pltpu.make_async_remote_copy(
            src_of(rows - 2), dst_of(0), send.at[*at, 0], recv.at[*at, 0],
            device_id={"rows": band + 1}, device_id_type=MESH)
        up = pltpu.make_async_remote_copy(
            src_of(0), dst_of(rows + 2), send.at[*at, 1], recv.at[*at, 1],
            device_id={"rows": band - 1}, device_id_type=MESH)
        return down, up

    def border_start(copies):
        down, up = copies

        @pl.when(has_down)
        def _():
            down.start()

        @pl.when(has_up)
        def _():
            up.start()

    def border_arrived(copies):
        down, up = copies

        @pl.when(has_up)
        def _():
            down.wait_recv()

        @pl.when(has_down)
        def _():
            up.wait_recv()

    def border_sent(copies):
        down, up = copies

        @pl.when(has_down)
        def _():
            down.wait_send()

        @pl.when(has_up)
        def _():
            up.wait_send()

    def input_border(which, f):
        src, dst = ((x_hbm, x1), (cot_hbm, xc))[which]
        half = slice((f % 2) * W, (f % 2 + 1) * W)
        return border(lambda r: src.at[f, r:r + 2], lambda r: dst.at[f // 2, r:r + 2, :, half], hs, hr, (which, f))

    def pair_border(buf, send, recv, p):
        return border(lambda r: buf.at[p, r + 2:r + 4], lambda r: buf.at[p, r:r + 2], send, recv, (p,))

    for f in (2, 3, 0, 1):
        border_start(input_border(0, f))

    def a_piece(i):
        lo, hi = PIECES[i]
        return pltpu.make_async_remote_copy(
            act2.at[2, lo:hi], act2.at[0, lo:hi], a_s.at[i], a_r.at[i], device_id={"tm": tm + 1}, device_id_type=MESH)

    def b_piece(i):
        lo, hi = BACK_PIECES[i]
        return pltpu.make_async_remote_copy(
            b3.at[0, lo:hi], b3.at[2, lo:hi], b_s.at[i], b_r.at[i], device_id={"tm": tm - 1}, device_id_type=MESH)

    def when_start(ok, copy):
        @pl.when(ok)
        def _():
            copy.start()

    def when_recv(ok, copy):
        @pl.when(ok)
        def _():
            copy.wait_recv()

    def when_sent(ok, copy):
        @pl.when(ok)
        def _():
            copy.wait_send()

    edge = jnp.zeros((2, C, 2 * W), bf16)

    def clear_rows(bufs):
        @pl.when(jnp.logical_not(has_up))
        def _():
            for buf in bufs:
                for p in range(2):
                    buf[p, 0:2] = edge

        @pl.when(jnp.logical_not(has_down))
        def _():
            for buf in bufs:
                for p in range(2):
                    buf[p, rows + 2:rows + 4] = edge

    def clear(ref, at):
        def one(r, _):
            ref[at, r] = edge[0]
            return 0
        lax.fori_loop(0, rows, one, 0)

    def clear_frames():
        @pl.when(jnp.logical_not(has_prev))
        def _():
            clear(act2, 0)

        @pl.when(jnp.logical_not(has_next))
        def _():
            clear(b3, 2)

    def arrange(n):
        for b in range(3):
            fw[n, b * C:(b + 1) * C, :] = jnp.concatenate(
                [kraw[n, a, b].astype(f32) for a in range(3)], axis=1).astype(bf16)

    def arrange_back(n):
        ref = bw1 if n == 0 else bw.at[n - 1]
        for b in range(3):
            ref[b * C:(b + 1) * C, :] = jnp.concatenate(
                [kraw[n, 2 - a, 2 - b].astype(f32).T for a in range(3)], axis=1).astype(bf16)

    def arrange_lags():
        lags = [traw[j].astype(f32) for j in range(3)]
        tf[...] = jnp.concatenate(lags, axis=1).astype(bf16)
        tb[...] = jnp.concatenate([k.T for k in lags[::-1]], axis=1).astype(bf16)

    def mid_one(p, lo, hi):
        def body(m):
            for s, v in zip(HALVES, conv_row(x1[p, pl.ds(m, 3)], fw[0])):
                act, slope = gelu_both(v)
                act1[p, m, :, s] = act.astype(bf16)
                sl1[p, m, :, s] = slope.astype(bf16)
        loop(lo, hi, body)

    def second(p, lo, hi):
        def body(r):
            for s, v in zip(HALVES, conv_row(act1[p, pl.ds(r, 3)], fw[1])):
                act, slope = gelu_both(v)
                act2[p + 1, r, :, s] = act.astype(bf16)
                sl2[p, r, :, s] = slope.astype(bf16)
        loop(lo, hi, body)

    def three(buf, first, r):
        early, late = buf[first, r], buf[first + 1, r]
        middle = jnp.concatenate([early[:, W:], late[:, :W]], axis=1)
        return early, middle, late

    def mix(p, lo, hi):
        def body(r):
            columns = jnp.concatenate(three(act2, p, r), axis=0)
            v = jnp.dot(tf[...], columns, preferred_element_type=f32)
            act, slope = gelu_both(v)
            x3[p, r + 2] = act.astype(bf16)
            sl3[p, r] = slope.astype(bf16)
        loop(lo, hi, body)

    def mid_four(p, lo, hi):
        def body(m):
            pre = conv_row(x3[p, pl.ds(m, 3)], fw[2])
            back = conv_row(xc[p, pl.ds(m, 3)], bw[2]) if p else [g4[m, :, s] for s in HALVES]
            for s, v, g in zip(HALVES, pre, back):
                act, slope = gelu_both(v)
                act4[p, m, :, s] = act.astype(bf16)
                bk4[p, m, :, s] = (g * slope).astype(bf16)
        loop(lo, hi, body)

    def back_cotangent(lo, hi):
        def body(m):
            for s, g in zip(HALVES, conv_row(xc[0, pl.ds(m, 3)], bw[2])):
                g4[m, :, s] = g
        loop(lo, hi, body)

    def decode(p, lo, hi):
        def body(r):
            for s, v in zip(HALVES, conv_row(act4[p, pl.ds(r, 3)], fw[3])):
                dec[p, r, :, s] = v.astype(bf16)
        loop(lo, hi, body)

    def back_three(p, lo, hi):
        def body(r):
            for s, g in zip(HALVES, conv_row(bk4[p, pl.ds(r, 3)], bw[1])):
                b3[p, r, :, s] = (g * sl3[p, r, :, s].astype(f32)).astype(bf16)
        loop(lo, hi, body)

    def unmix(p, lo, hi):
        def body(r):
            columns = jnp.concatenate(three(b3, p, r), axis=0)
            g = jnp.dot(tb[...], columns, preferred_element_type=f32)
            x5[p, r + 2] = (g * sl2[p, r].astype(f32)).astype(bf16)
        loop(lo, hi, body)

    def back_one(p, lo, hi):
        bk1 = (bk1_early, bk1_late)[p]

        def body(m):
            for s, g in zip(HALVES, conv_row(x5[p, pl.ds(m, 3)], bw[0])):
                bk1[m, :, s] = (g * sl1[p, m, :, s].astype(f32)).astype(bf16)
        loop(lo, hi, body)

    def grads(lo, hi):
        def body(r):
            for s, g in zip(HALVES, conv_row(bk1_early[pl.ds(r, 3)], bw1[...])):
                grad0[r, :, s] = g
        loop(lo, hi, body)

    def outside_first(p, bufs):
        @pl.when(jnp.logical_not(has_up))
        def _():
            for buf in bufs:
                buf[p, 0] = edge[0]

    def outside_last(p, bufs):
        @pl.when(jnp.logical_not(has_down))
        def _():
            for buf in bufs:
                buf[p, rows + 1] = edge[0]

    def outside(p, bufs):
        outside_first(p, bufs)
        outside_last(p, bufs)

    def edges(step, p, extra=0):
        step(p, 0, 2)
        step(p, rows - 2 + extra, rows + extra)

    def input_arrived(which, p):
        for f in (2 * p, 2 * p + 1):
            border_arrived(input_border(which, f))

    w_copies[0].wait()
    arrange(0)
    for f in (2, 3):
        load(0, f).wait()
    mid_one(1, 2, rows)
    w_copies[1].wait()
    arrange(1)
    second(1, 2, 6)
    when_start(has_next, a_piece(0))
    second(1, 6, rows - 2)
    for f in (0, 1):
        load(0, f).wait()
    mid_one(0, 2, rows)
    second(0, 2, rows - 2)
    clear_rows((x1,))
    input_arrived(0, 1)
    edges(mid_one, 1, 2)
    outside(1, (act1, sl1))
    edges(second, 1)
    for i in (1, 2):
        when_start(has_next, a_piece(i))
    for f in (2, 3, 0, 1):
        border_start(input_border(1, f))
    for i in (3, 4):
        when_start(has_next, a_piece(i))
    input_arrived(0, 0)
    edges(mid_one, 0, 2)
    outside(0, (act1, sl1))
    edges(second, 0)
    for i in (2, 3, 4):
        w_copies[i].wait()
    arrange_lags()
    edges(mix, 1)
    border_start(pair_border(x3, x3s, x3r, 1))
    mix(1, 2, rows - 2)

    clear_rows((xc, x3, x5))
    for f in (2, 3, 0, 1):
        load(1, f).wait()
        border_arrived(input_border(1, f))
    arrange(2)
    arrange_back(3)
    back_cotangent(0, rows + 2)
    mid_four(1, 2, rows)
    clear_frames()
    for i in (1, 2):
        when_recv(has_prev, a_piece(i))
        mix(0, *PIECES[i])
    border_start(pair_border(x3, x3s, x3r, 0))
    arrange_back(2)
    back_three(1, 2, rows - 2)
    border_arrived(pair_border(x3, x3s, x3r, 1))
    edges(mid_four, 1, 2)
    outside(1, (act4, bk4))
    edges(back_three, 1)
    arrange(3)
    decode(1, 0, rows)
    arrange_back(1)
    arrange_back(0)
    when_recv(has_prev, a_piece(0))
    mix(0, *PIECES[0])
    when_recv(has_prev, a_piece(3))
    mix(0, *PIECES[3])
    mid_four(0, 2, 10)
    border_arrived(pair_border(x3, x3s, x3r, 0))
    mid_four(0, 0, 2)
    outside_first(0, (act4, bk4))
    for i in (0, 1):
        back_three(0, *BACK_PIECES[i])
        when_start(has_prev, b_piece(i))
    when_recv(has_prev, a_piece(4))
    mix(0, *PIECES[4])
    mid_four(0, 10, rows + 2)
    outside_last(0, (act4, bk4))
    for i in (2, 3, 4):
        back_three(0, *BACK_PIECES[i])
        when_start(has_prev, b_piece(i))
    edges(unmix, 0)
    border_start(pair_border(x5, x5s, x5r, 0))
    unmix(0, 2, rows - 2)
    decode(0, 0, rows)
    back_one(0, 2, rows)
    grads(2, rows - 2)
    border_arrived(pair_border(x5, x5s, x5r, 0))
    edges(back_one, 0, 2)
    grads(0, 2)
    grads(rows - 2, rows)

    for i in (0, 1, 2):
        when_recv(has_next, b_piece(i))
        unmix(1, *BACK_PIECES[i])
    border_start(pair_border(x5, x5s, x5r, 1))
    when_recv(has_next, b_piece(3))
    unmix(1, *BACK_PIECES[3])
    back_one(1, 2, 11)
    when_recv(has_next, b_piece(4))
    unmix(1, *BACK_PIECES[4])
    back_one(1, 11, rows)
    border_arrived(pair_border(x5, x5s, x5r, 1))
    edges(back_one, 1, 2)

    for which in range(2):
        for f in range(4):
            border_sent(input_border(which, f))
    for p in range(2):
        border_sent(pair_border(x3, x3s, x3r, p))
        border_sent(pair_border(x5, x5s, x5r, p))
    for i in range(len(PIECES)):
        when_sent(has_next, a_piece(i))
        when_sent(has_prev, b_piece(i))


def per_device(sizes, frames_in, conv_one, conv_two, temporal, conv_three, conv_four, cotangent):
    frames, rows = frames_in.shape[:2]
    sizes = (*sizes, rows)
    taps = [jnp.transpose(k, (1, 2, 0, 3)) for k in (conv_one, conv_two, conv_three, conv_four)]
    bf16, f32 = jnp.bfloat16, jnp.float32

    def pair(extra, count=2):
        return pltpu.VMEM((count, rows + extra, C, 2 * W), bf16)

    dma = pltpu.SemaphoreType.DMA
    hbm, vmem = pl.BlockSpec(memory_space=pltpu.HBM), pl.BlockSpec(memory_space=pltpu.VMEM)
    matrix = (3 * C, 3 * C)
    halfway = pl.pallas_call(
        functools.partial(kernel, sizes),
        name="stack",
        out_shape=(
            jax.ShapeDtypeStruct((2, rows, C, 2 * W), bf16),
            jax.ShapeDtypeStruct((rows, C, 2 * W), f32),
            jax.ShapeDtypeStruct((rows + 2, C, 2 * W), bf16),
            jax.ShapeDtypeStruct(matrix, bf16),
        ),
        in_specs=[hbm] * 7,
        out_specs=(vmem,) * 4,
        scratch_shapes=[
            pair(4), pair(4), pair(4), pair(4),
            pair(2), pair(2),
            pair(0, count=3), pair(0), pair(0),
            pair(2), pair(2), pltpu.VMEM((rows + 2, C, 2 * W), f32),
            pair(0, count=3),
            pltpu.VMEM((rows + 2, C, 2 * W), bf16),
            pltpu.VMEM((4, *matrix), bf16), pltpu.VMEM((3, *matrix), bf16),
            pltpu.VMEM((C, 3 * C), bf16), pltpu.VMEM((C, 3 * C), bf16),
            pltpu.VMEM((4, 3, 3, C, C), bf16), pltpu.VMEM((3, C, C), bf16),
            dma((5,)), dma((2, 4)),
            dma((2, 4, 2)), dma((2, 4, 2)),
            dma((2, 2)), dma((2, 2)), dma((2, 2)), dma((2, 2)),
            dma((5,)), dma((5,)), dma((5,)), dma((5,)),
        ],
        compiler_params=pltpu.CompilerParams(collective_id=0, has_side_effects=True, vmem_limit_bytes=36 << 20),
    )(*[pltpu.with_memory_space_constraint(v, pltpu.HBM) for v in (frames_in, taps[0], taps[1], temporal, taps[2], taps[3], cotangent)])
    return pl.pallas_call(
        functools.partial(last_kernel, rows),
        name="last",
        out_shape=(jax.ShapeDtypeStruct(frames_in.shape, bf16), jax.ShapeDtypeStruct(frames_in.shape, f32)),
        in_specs=[vmem] * 4,
        out_specs=(hbm, hbm),
        scratch_shapes=[pltpu.VMEM((rows, C, 2 * W), f32), dma((2, 4))],
        compiler_params=pltpu.CompilerParams(vmem_limit_bytes=16 << 20),
    )(*halfway)


def solution(mesh):
    split = P("tm", "rows", None, None)
    return jax.shard_map(
        functools.partial(per_device, (mesh.shape["tm"], mesh.shape["rows"])),
        mesh=mesh,
        in_specs=(split, P(), P(), P(), P(), P(), split),
        out_specs=(split, split),
        check_vma=False,
    )
```

```python
import functools

import jax
import jax.numpy as jnp
from jax import lax
from jax.experimental import pallas as pl
from jax.experimental.pallas import tpu as pltpu
from jax.sharding import PartitionSpec as P

SQRT_HALF = 0.7071067811865476
INV_ROOT_TAU = 0.3989422804014327
MESH = pl.DeviceIdType.MESH
C = 64
W = 128
PIECES = ((2, 6), (0, 2), (14, 16), (6, 10), (10, 14))
BACK_PIECES = ((0, 4), (4, 8), (14, 16), (8, 11), (11, 14))


def gelu_both(v):
    phi = 0.5 + 0.5 * lax.erf(v * SQRT_HALF)
    bump = jnp.exp(v * v * -0.5) * INV_ROOT_TAU
    return v * phi, phi + v * bump


def conv_row(window, weights):
    lane = lax.broadcasted_iota(jnp.int32, (C, W), 1)
    y = jnp.dot(weights, window.reshape(3 * C, 2 * W), preferred_element_type=jnp.float32)
    out = []
    for q in range(2):
        part = y[:, q * W:(q + 1) * W]
        left = jnp.where(lane == 0, 0.0, pltpu.roll(part[0:C], 1, 1))
        right = jnp.where(lane == W - 1, 0.0, pltpu.roll(part[2 * C:], W - 1, 1))
        out.append(left + part[C:2 * C] + right)
    return out


HALVES = (slice(0, W), slice(W, 2 * W))


def loop(lo, hi, body):
    def one(r, _):
        body(r)
        return 0
    lax.fori_loop(lo, hi, one, 0, unroll=hi - lo)


def last_kernel(rows, dec, grad0, bk1, bw1, dec_hbm, grad_hbm, grad1, sem):
    def store(which, f):
        src, dst = ((dec.at[f // 2], dec_hbm), ((grad0, grad1)[f // 2], grad_hbm))[which]
        return pltpu.make_async_copy(src.at[:, :, HALVES[f % 2]], dst.at[f], sem.at[which, f])

    for which, f in ((0, 0), (0, 1), (0, 2), (0, 3), (1, 0), (1, 1)):
        store(which, f).start()

    def body(r):
        for s, g in zip(HALVES, conv_row(bk1[pl.ds(r, 3)], bw1[...])):
            grad1[r, :, s] = g
    loop(0, rows, body)
    for f in (2, 3):
        store(1, f).start()
    for which in range(2):
        for f in range(4):
            store(which, f).wait()


def kernel(sizes, x_hbm, k1, k2, t_hbm, k3, k4, cot_hbm, dec, grad0, bk1_late, bw1,
           x1, xc, x3, x5, act1, sl1, act2, sl2, sl3, act4, bk4, g4, b3, bk1_early, fw, bw, tf, tb, kraw, traw,
           w_sem, in_sem, hs, hr, x3s, x3r, x5s, x5r, a_s, a_r, b_s, b_r):
    n_tm, n_rows, rows = sizes
    tm = lax.axis_index("tm")
    band = lax.axis_index("rows")
    has_up, has_down = band > 0, band < n_rows - 1
    has_prev, has_next = tm > 0, tm < n_tm - 1
    bf16, f32 = jnp.bfloat16, jnp.float32

    w_copies = [pltpu.make_async_copy(k, kraw.at[i], w_sem.at[i]) for i, k in enumerate((k1, k2, k3, k4))]
    w_copies.append(pltpu.make_async_copy(t_hbm, traw, w_sem.at[4]))
    for c in w_copies:
        c.start()

    def load(which, f):
        src, dst = ((x_hbm, x1), (cot_hbm, xc))[which]
        return pltpu.make_async_copy(
            src.at[f], dst.at[f // 2, 2:rows + 2, :, (f % 2) * W:(f % 2 + 1) * W], in_sem.at[which, f])

    for which, f in ((0, 2), (0, 3), (0, 0), (0, 1), (1, 2), (1, 3), (1, 0), (1, 1)):
        load(which, f).start()

    barrier = pltpu.get_barrier_semaphore()
    count = jnp.int32(0)
    for ok, peer in ((has_up, {"rows": band - 1}), (has_down, {"rows": band + 1}),
                     (has_prev, {"tm": tm - 1}), (has_next, {"tm": tm + 1})):
        @pl.when(ok)
        def _():
            pl.semaphore_signal(barrier, inc=1, device_id=peer, device_id_type=MESH)
        count = count + ok.astype(jnp.int32)
    pl.semaphore_wait(barrier, count)

    def border(src_of, dst_of, send, recv, at):
        down = pltpu.make_async_remote_copy(
            src_of(rows - 2), dst_of(0), send.at[*at, 0], recv.at[*at, 0],
            device_id={"rows": band + 1}, device_id_type=MESH)
        up = pltpu.make_async_remote_copy(
            src_of(0), dst_of(rows + 2), send.at[*at, 1], recv.at[*at, 1],
            device_id={"rows": band - 1}, device_id_type=MESH)
        return down, up

    def border_start(copies):
        down, up = copies

        @pl.when(has_down)
        def _():
            down.start()

        @pl.when(has_up)
        def _():
            up.start()

    def border_arrived(copies):
        down, up = copies

        @pl.when(has_up)
        def _():
            down.wait_recv()

        @pl.when(has_down)
        def _():
            up.wait_recv()

    def border_sent(copies):
        down, up = copies

        @pl.when(has_down)
        def _():
            down.wait_send()

        @pl.when(has_up)
        def _():
            up.wait_send()

    def input_border(which, f):
        src, dst = ((x_hbm, x1), (cot_hbm, xc))[which]
        half = slice((f % 2) * W, (f % 2 + 1) * W)
        return border(lambda r: src.at[f, r:r + 2], lambda r: dst.at[f // 2, r:r + 2, :, half], hs, hr, (which, f))

    def pair_border(buf, send, recv, p):
        return border(lambda r: buf.at[p, r + 2:r + 4], lambda r: buf.at[p, r:r + 2], send, recv, (p,))

    for f in (2, 3, 0, 1):
        border_start(input_border(0, f))

    def a_piece(i):
        lo, hi = PIECES[i]
        return pltpu.make_async_remote_copy(
            act2.at[2, lo:hi], act2.at[0, lo:hi], a_s.at[i], a_r.at[i], device_id={"tm": tm + 1}, device_id_type=MESH)

    def b_piece(i):
        lo, hi = BACK_PIECES[i]
        return pltpu.make_async_remote_copy(
            b3.at[0, lo:hi], b3.at[2, lo:hi], b_s.at[i], b_r.at[i], device_id={"tm": tm - 1}, device_id_type=MESH)

    def when_start(ok, copy):
        @pl.when(ok)
        def _():
            copy.start()

    def when_recv(ok, copy):
        @pl.when(ok)
        def _():
            copy.wait_recv()

    def when_sent(ok, copy):
        @pl.when(ok)
        def _():
            copy.wait_send()

    edge = jnp.zeros((2, C, 2 * W), bf16)

    def clear_rows(bufs):
        @pl.when(jnp.logical_not(has_up))
        def _():
            for buf in bufs:
                for p in range(2):
                    buf[p, 0:2] = edge

        @pl.when(jnp.logical_not(has_down))
        def _():
            for buf in bufs:
                for p in range(2):
                    buf[p, rows + 2:rows + 4] = edge

    def clear(ref, at):
        def one(r, _):
            ref[at, r] = edge[0]
            return 0
        lax.fori_loop(0, rows, one, 0)

    def clear_frames():
        @pl.when(jnp.logical_not(has_prev))
        def _():
            clear(act2, 0)

        @pl.when(jnp.logical_not(has_next))
        def _():
            clear(b3, 2)

    def arrange(n):
        for b in range(3):
            fw[n, b * C:(b + 1) * C, :] = jnp.concatenate(
                [kraw[n, a, b].astype(f32) for a in range(3)], axis=1).astype(bf16)

    def arrange_back(n):
        ref = bw1 if n == 0 else bw.at[n - 1]
        for b in range(3):
            ref[b * C:(b + 1) * C, :] = jnp.concatenate(
                [kraw[n, 2 - a, 2 - b].astype(f32).T for a in range(3)], axis=1).astype(bf16)

    def arrange_lags():
        lags = [traw[j].astype(f32) for j in range(3)]
        tf[...] = jnp.concatenate(lags, axis=1).astype(bf16)
        tb[...] = jnp.concatenate([k.T for k in lags[::-1]], axis=1).astype(bf16)

    def mid_one(p, lo, hi):
        def body(m):
            for s, v in zip(HALVES, conv_row(x1[p, pl.ds(m, 3)], fw[0])):
                act, slope = gelu_both(v)
                act1[p, m, :, s] = act.astype(bf16)
                sl1[p, m, :, s] = slope.astype(bf16)
        loop(lo, hi, body)

    def second(p, lo, hi):
        def body(r):
            for s, v in zip(HALVES, conv_row(act1[p, pl.ds(r, 3)], fw[1])):
                act, slope = gelu_both(v)
                act2[p + 1, r, :, s] = act.astype(bf16)
                sl2[p, r, :, s] = slope.astype(bf16)
        loop(lo, hi, body)

    def three(buf, first, r):
        early, late = buf[first, r], buf[first + 1, r]
        middle = jnp.concatenate([early[:, W:], late[:, :W]], axis=1)
        return early, middle, late

    def mix(p, lo, hi):
        def body(r):
            columns = jnp.concatenate(three(act2, p, r), axis=0)
            v = jnp.dot(tf[...], columns, preferred_element_type=f32)
            act, slope = gelu_both(v)
            x3[p, r + 2] = act.astype(bf16)
            sl3[p, r] = slope.astype(bf16)
        loop(lo, hi, body)

    def mid_four(p, lo, hi):
        def body(m):
            pre = conv_row(x3[p, pl.ds(m, 3)], fw[2])
            back = conv_row(xc[p, pl.ds(m, 3)], bw[2]) if p else [g4[m, :, s] for s in HALVES]
            for s, v, g in zip(HALVES, pre, back):
                act, slope = gelu_both(v)
                act4[p, m, :, s] = act.astype(bf16)
                bk4[p, m, :, s] = (g * slope).astype(bf16)
        loop(lo, hi, body)

    def back_cotangent(lo, hi):
        def body(m):
            for s, g in zip(HALVES, conv_row(xc[0, pl.ds(m, 3)], bw[2])):
                g4[m, :, s] = g
        loop(lo, hi, body)

    def decode(p, lo, hi):
        def body(r):
            for s, v in zip(HALVES, conv_row(act4[p, pl.ds(r, 3)], fw[3])):
                dec[p, r, :, s] = v.astype(bf16)
        loop(lo, hi, body)

    def back_three(p, lo, hi):
        def body(r):
            for s, g in zip(HALVES, conv_row(bk4[p, pl.ds(r, 3)], bw[1])):
                b3[p, r, :, s] = (g * sl3[p, r, :, s].astype(f32)).astype(bf16)
        loop(lo, hi, body)

    def unmix(p, lo, hi):
        def body(r):
            columns = jnp.concatenate(three(b3, p, r), axis=0)
            g = jnp.dot(tb[...], columns, preferred_element_type=f32)
            x5[p, r + 2] = (g * sl2[p, r].astype(f32)).astype(bf16)
        loop(lo, hi, body)

    def back_one(p, lo, hi):
        bk1 = (bk1_early, bk1_late)[p]

        def body(m):
            for s, g in zip(HALVES, conv_row(x5[p, pl.ds(m, 3)], bw[0])):
                bk1[m, :, s] = (g * sl1[p, m, :, s].astype(f32)).astype(bf16)
        loop(lo, hi, body)

    def grads(lo, hi):
        def body(r):
            for s, g in zip(HALVES, conv_row(bk1_early[pl.ds(r, 3)], bw1[...])):
                grad0[r, :, s] = g
        loop(lo, hi, body)

    def outside_first(p, bufs):
        @pl.when(jnp.logical_not(has_up))
        def _():
            for buf in bufs:
                buf[p, 0] = edge[0]

    def outside_last(p, bufs):
        @pl.when(jnp.logical_not(has_down))
        def _():
            for buf in bufs:
                buf[p, rows + 1] = edge[0]

    def outside(p, bufs):
        outside_first(p, bufs)
        outside_last(p, bufs)

    def edges(step, p, extra=0):
        step(p, 0, 2)
        step(p, rows - 2 + extra, rows + extra)

    def input_arrived(which, p):
        for f in (2 * p, 2 * p + 1):
            border_arrived(input_border(which, f))

    w_copies[0].wait()
    arrange(0)
    for f in (2, 3):
        load(0, f).wait()
    mid_one(1, 2, rows)
    w_copies[1].wait()
    arrange(1)
    second(1, 2, 6)
    when_start(has_next, a_piece(0))
    second(1, 6, rows - 2)
    for f in (0, 1):
        load(0, f).wait()
    mid_one(0, 2, rows)
    second(0, 2, rows - 2)
    clear_rows((x1,))
    input_arrived(0, 1)
    edges(mid_one, 1, 2)
    outside(1, (act1, sl1))
    edges(second, 1)
    for i in (1, 2):
        when_start(has_next, a_piece(i))
    for f in (2, 3, 0, 1):
        border_start(input_border(1, f))
    for i in (3, 4):
        when_start(has_next, a_piece(i))
    input_arrived(0, 0)
    edges(mid_one, 0, 2)
    outside(0, (act1, sl1))
    edges(second, 0)
    for i in (2, 3, 4):
        w_copies[i].wait()
    arrange_lags()
    edges(mix, 1)
    border_start(pair_border(x3, x3s, x3r, 1))
    mix(1, 2, rows - 2)

    clear_rows((xc, x3, x5))
    for f in (2, 3, 0, 1):
        load(1, f).wait()
    arrange(2)
    arrange_back(3)
    back_cotangent(2, rows)
    mid_four(1, 2, rows)
    clear_frames()
    for i in (1, 2):
        when_recv(has_prev, a_piece(i))
        mix(0, *PIECES[i])
    border_start(pair_border(x3, x3s, x3r, 0))
    arrange_back(2)
    back_three(1, 2, rows - 2)
    input_arrived(1, 0)
    back_cotangent(0, 2)
    back_cotangent(rows, rows + 2)
    when_recv(has_prev, a_piece(0))
    mix(0, *PIECES[0])
    when_recv(has_prev, a_piece(3))
    mix(0, *PIECES[3])
    mid_four(0, 2, 10)
    border_arrived(pair_border(x3, x3s, x3r, 0))
    mid_four(0, 0, 2)
    outside_first(0, (act4, bk4))
    for i in (0, 1):
        back_three(0, *BACK_PIECES[i])
    when_recv(has_prev, a_piece(4))
    for i in (0, 1):
        when_start(has_prev, b_piece(i))
    mix(0, *PIECES[4])
    mid_four(0, 10, rows + 2)
    outside_last(0, (act4, bk4))
    for i in (2, 3, 4):
        back_three(0, *BACK_PIECES[i])
        when_start(has_prev, b_piece(i))
    input_arrived(1, 1)
    border_arrived(pair_border(x3, x3s, x3r, 1))
    edges(mid_four, 1, 2)
    outside(1, (act4, bk4))
    edges(back_three, 1)
    edges(unmix, 0)
    border_start(pair_border(x5, x5s, x5r, 0))
    unmix(0, 2, rows - 2)
    arrange_back(1)
    arrange_back(0)
    arrange(3)
    decode(1, 0, rows)
    decode(0, 0, rows)
    back_one(0, 2, rows)
    grads(2, rows - 2)
    border_arrived(pair_border(x5, x5s, x5r, 0))
    edges(back_one, 0, 2)
    grads(0, 2)
    grads(rows - 2, rows)

    for i in (0, 1, 2):
        when_recv(has_next, b_piece(i))
        unmix(1, *BACK_PIECES[i])
    border_start(pair_border(x5, x5s, x5r, 1))
    when_recv(has_next, b_piece(3))
    unmix(1, *BACK_PIECES[3])
    back_one(1, 2, 11)
    when_recv(has_next, b_piece(4))
    unmix(1, *BACK_PIECES[4])
    back_one(1, 11, rows)
    border_arrived(pair_border(x5, x5s, x5r, 1))
    edges(back_one, 1, 2)

    for which in range(2):
        for f in range(4):
            border_sent(input_border(which, f))
    for p in range(2):
        border_sent(pair_border(x3, x3s, x3r, p))
        border_sent(pair_border(x5, x5s, x5r, p))
    for i in range(len(PIECES)):
        when_sent(has_next, a_piece(i))
        when_sent(has_prev, b_piece(i))


def per_device(sizes, frames_in, conv_one, conv_two, temporal, conv_three, conv_four, cotangent):
    frames, rows = frames_in.shape[:2]
    sizes = (*sizes, rows)
    taps = [jnp.transpose(k, (1, 2, 0, 3)) for k in (conv_one, conv_two, conv_three, conv_four)]
    bf16, f32 = jnp.bfloat16, jnp.float32

    def pair(extra, count=2):
        return pltpu.VMEM((count, rows + extra, C, 2 * W), bf16)

    dma = pltpu.SemaphoreType.DMA
    hbm, vmem = pl.BlockSpec(memory_space=pltpu.HBM), pl.BlockSpec(memory_space=pltpu.VMEM)
    matrix = (3 * C, 3 * C)
    halfway = pl.pallas_call(
        functools.partial(kernel, sizes),
        name="stack",
        out_shape=(
            jax.ShapeDtypeStruct((2, rows, C, 2 * W), bf16),
            jax.ShapeDtypeStruct((rows, C, 2 * W), f32),
            jax.ShapeDtypeStruct((rows + 2, C, 2 * W), bf16),
            jax.ShapeDtypeStruct(matrix, bf16),
        ),
        in_specs=[hbm] * 7,
        out_specs=(vmem,) * 4,
        scratch_shapes=[
            pair(4), pair(4), pair(4), pair(4),
            pair(2), pair(2),
            pair(0, count=3), pair(0), pair(0),
            pair(2), pair(2), pltpu.VMEM((rows + 2, C, 2 * W), f32),
            pair(0, count=3),
            pltpu.VMEM((rows + 2, C, 2 * W), bf16),
            pltpu.VMEM((4, *matrix), bf16), pltpu.VMEM((3, *matrix), bf16),
            pltpu.VMEM((C, 3 * C), bf16), pltpu.VMEM((C, 3 * C), bf16),
            pltpu.VMEM((4, 3, 3, C, C), bf16), pltpu.VMEM((3, C, C), bf16),
            dma((5,)), dma((2, 4)),
            dma((2, 4, 2)), dma((2, 4, 2)),
            dma((2, 2)), dma((2, 2)), dma((2, 2)), dma((2, 2)),
            dma((5,)), dma((5,)), dma((5,)), dma((5,)),
        ],
        compiler_params=pltpu.CompilerParams(collective_id=0, has_side_effects=True, vmem_limit_bytes=36 << 20),
    )(*[pltpu.with_memory_space_constraint(v, pltpu.HBM) for v in (frames_in, taps[0], taps[1], temporal, taps[2], taps[3], cotangent)])
    return pl.pallas_call(
        functools.partial(last_kernel, rows),
        name="last",
        out_shape=(jax.ShapeDtypeStruct(frames_in.shape, bf16), jax.ShapeDtypeStruct(frames_in.shape, f32)),
        in_specs=[vmem] * 4,
        out_specs=(hbm, hbm),
        scratch_shapes=[pltpu.VMEM((rows, C, 2 * W), f32), dma((2, 4))],
        compiler_params=pltpu.CompilerParams(vmem_limit_bytes=16 << 20),
    )(*halfway)


def solution(mesh):
    split = P("tm", "rows", None, None)
    return jax.shard_map(
        functools.partial(per_device, (mesh.shape["tm"], mesh.shape["rows"])),
        mesh=mesh,
        in_specs=(split, P(), P(), P(), P(), P(), split),
        out_specs=(split, split),
        check_vma=False,
    )
```
